32 devices in a mesh: dp: 16 (over z, y, core), tensor: 2 (over x).
Axes of the slice: x: 2, y: 2, z: 4, core: 2. Of those that a mesh axis runs over, the one named last changes fastest.
Arguments:
- tokens: bfloat16 [28672, 768], P(('dp', 'tensor')), may hold values from -6 to 6
- cotangent: bfloat16 [28672, 768], P(('dp', 'tensor')), may hold values from -6 to 6
- time_embed: float32 [16, 128], P('dp'), may hold values from -4 to 4
- block_parent: int32 [16, 14], P('dp'), may hold values from 0 to 5, as said below
- positions: int32 [28672], P('dp'), may hold values from 0 to 511, as said below
- gain_first: bfloat16 [768], P(('dp', 'tensor')), may hold values from 0.25 to 1.75
- inlet_weight: bfloat16 [768, 3, 12, 64], P('dp', None, 'tensor'), may hold values from -0.21875 to 0.21875
- outlet_weight: bfloat16 [12, 64, 768], P('tensor', None, 'dp'), may hold values from -0.875 to 0.875
- gain_second: bfloat16 [768], P(('dp', 'tensor')), may hold values from 0.25 to 1.75
- up_weight: bfloat16 [768, 3072], P(None, ('dp', 'tensor')), may hold values from -0.21875 to 0.21875
- up_bias: bfloat16 [3072], P(('dp', 'tensor')), may hold values from -3 to 3
- down_weight: bfloat16 [3072, 768], P(('dp', 'tensor')), may hold values from -0.109375 to 0.109375
- down_bias: bfloat16 [768], P(('dp', 'tensor')), may hold values from -2 to 2
- modulator: bfloat16 [128, 6, 768], P(None, None, ('dp', 'tensor')), may hold values from -0.5 to 0.5
- modulator_bias: bfloat16 [6, 768], P(None, ('dp', 'tensor')), may hold values from -3 to 3
Outputs:
- layer_output: bfloat16 [28672, 768], P(('dp', 'tensor'))
- adjoint_tokens: bfloat16 [28672, 768], P(('dp', 'tensor'))
- adjoint_gain_first: float32 [768], P(('dp', 'tensor'))
- adjoint_inlet: float32 [768, 3, 12, 64], P('dp', None, 'tensor')
- adjoint_outlet: float32 [12, 64, 768], P('tensor', None, 'dp')
- adjoint_gain_second: float32 [768], P(('dp', 'tensor'))
- adjoint_up_weight: float32 [768, 3072], P(None, ('dp', 'tensor'))
- adjoint_up_bias: float32 [3072], P(('dp', 'tensor'))
- adjoint_down_weight: float32 [3072, 768], P(('dp', 'tensor'))
- adjoint_down_bias: float32 [768], P(('dp', 'tensor'))
- adjoint_modulator: float32 [128, 6, 768], P(None, None, ('dp', 'tensor'))
- adjoint_modulator_bias: float32 [6, 768], P(None, ('dp', 'tensor'))
The draws below stay inside these ranges and needn't reach their ends.
Inputs may be any that keep to these rules, and one draw needn't show every extreme that they name: block_parent[t, b] is the parent block of block b of tree t. Blocks 0 to 1 are the trunk: block 0 is its own parent and block b > 0 has parent b - 1. The next 4 blocks are branches, each with a trunk block as parent; the last 8 blocks are leaves, each with a branch block as parent. positions of a token = 128 times the number of strict ancestors of its block plus its place within its block.
All inputs are finite; a program needn't handle non-finite values.
Results may differ from the reference program's by a relative error of at most 0.02.
The reference program's roundings to bfloat16 on the way count: a program that leaves them out, or rounds other values in their place, can miss the bound.
Values may be sent and summed in bfloat16 or wider, within the bound.
No kernel may reach another device: no remote copies, remote signals or barrier semaphores. Data moves between devices by JAX's collectives and lax.ppermute only.
A program may use at most 192 MiB of HBM per device.

```python
import jax
import jax.numpy as jnp
from jax import lax

D = 768
H = 12
FF = 3072
C = 128
BLK = 128
TRUNK_BLKS = 2
BRANCHES = 4
LEAVES = 2
HD = 64
SEQ = 1792
TREES = 16
TOKENS = 28672


def tree_shape(key):
    shape_key = jax.random.fold_in(key, 4242)
    fork_points = jax.random.randint(jax.random.fold_in(shape_key, 1), (TREES, BRANCHES), 0, TRUNK_BLKS)
    leaf_homes = jax.random.randint(jax.random.fold_in(shape_key, 2), (TREES, BRANCHES * LEAVES), 0, BRANCHES)
    fork_points = fork_points.at[0, BRANCHES - 1].set(TRUNK_BLKS - 1).astype(jnp.int32)
    leaf_homes = leaf_homes.at[0, 0].set(BRANCHES - 1).astype(jnp.int32)
    trunk_links = jnp.maximum(jnp.arange(TRUNK_BLKS, dtype=jnp.int32) - 1, 0)
    trunk_rows = jnp.broadcast_to(trunk_links[None, :], (TREES, TRUNK_BLKS))
    parents = jnp.concatenate([trunk_rows, fork_points, leaf_homes + TRUNK_BLKS], axis=1)
    return (parents.astype(jnp.int32), fork_points, leaf_homes)


def draw_block_parent(key, part):
    return tree_shape(key)[0]


def draw_positions(key, part):
    parents, fork_points, leaf_homes = tree_shape(key)
    branch_depth = fork_points + 1
    leaf_depth = jnp.take_along_axis(branch_depth, leaf_homes, axis=1) + 1
    trunk_depth = jnp.broadcast_to(jnp.arange(TRUNK_BLKS, dtype=jnp.int32)[None, :], (TREES, TRUNK_BLKS))
    depth = jnp.concatenate([trunk_depth, branch_depth, leaf_depth], axis=1)
    places = depth[:, :, None] * BLK + jnp.arange(BLK, dtype=jnp.int32)[None, None, :]
    return places.reshape(TREES * SEQ).astype(jnp.int32)


def strengthened(array, stream_key, source, target, parts, factor):
    def block_of(dim):
        return (jnp.arange(array.shape[dim]) // (array.shape[dim] // parts)).reshape((-1,) + (1,) * (array.ndim - 1 - dim))

    first = jax.random.permutation(stream_key, parts)[block_of(target)]
    other_side = (block_of(target) + parts // 2) % parts
    return jnp.where((block_of(source) == first) | (block_of(source) == other_side), factor * array, array)


def steps_of(rng, extent, cuts, smallest, largest):
    def one(dim, parts):
        draws = jax.random.uniform(jax.random.fold_in(jax.random.fold_in(rng, 6), dim), (parts,), jnp.float32, smallest / len(cuts), largest / len(cuts))
        return jnp.repeat(jnp.exp(draws), extent[dim] // parts).reshape((-1,) + (1,) * (len(extent) - dim - 1))

    loudness = one(*cuts[0])
    for cut in cuts[1:]:
        loudness = loudness * one(*cut)
    return loudness


def noise(stream_key, dims, scale, most, pieces=(), held_as=jnp.bfloat16):
    values = scale * jax.random.normal(stream_key, dims, jnp.float32)
    if pieces:
        values = values * steps_of(stream_key, dims, pieces, -0.22, 0.18)
    return jnp.clip(values, -most, most).astype(held_as)


def noise_with(own_key, dims, scale, reach, pieces, heavy, kind=jnp.bfloat16):
    entries = scale * jax.random.normal(own_key, dims, jnp.float32)
    if pieces:
        entries = entries * steps_of(own_key, dims, pieces, -0.22, 0.18)
    return jnp.clip(strengthened(entries, jax.random.fold_in(own_key, 3), *heavy), -reach, reach).astype(kind)


def setup_inputs(seed: int = 0) -> dict:
    streams_of = jax.random.split(jax.random.key(seed), 16)
    return {
        "tokens": noise(streams_of[0], (TOKENS, D), 1.0, 6.0, ((0, 32),)),
        "cotangent": noise_with(streams_of[1], (TOKENS, D), 1.0, 6.0, ((0, 32),), (0, 1, 32, 2.75)),
        "time_embed": noise(streams_of[2], (TREES, C), 1.0, 4.0, ((0, 16),), jnp.float32),
        "block_parent": draw_block_parent(jax.random.fold_in(streams_of[15], 71), 0),
        "positions": draw_positions(jax.random.fold_in(streams_of[15], 71), 0),
        "gain_first": jnp.clip(1.0 + 0.15 * jax.random.normal(streams_of[5], (D,), jnp.float32), 0.25, 1.75).astype(jnp.bfloat16),
        "inlet_weight": noise(streams_of[6], (D, 3, H, HD), D ** -0.5, 0.21875, ((0, 16), (2, 2))),
        "outlet_weight": noise(streams_of[7], (H, HD, D), (D // 16) ** -0.5, 0.875, ((0, 2), (2, 16))),
        "gain_second": jnp.clip(1.0 + 0.15 * jax.random.normal(streams_of[8], (D,), jnp.float32), 0.25, 1.75).astype(jnp.bfloat16),
        "up_weight": noise(streams_of[9], (D, FF), D ** -0.5, 0.21875, ((1, 32),)),
        "up_bias": noise(streams_of[10], (FF,), 0.5, 3.0, ((0, 32),)),
        "down_weight": noise(streams_of[11], (FF, D), FF ** -0.5, 0.109375, ((0, 32),)),
        "down_bias": noise(streams_of[12], (D,), 0.3, 2.0, ((0, 32),)),
        "modulator": noise(streams_of[13], (C, 6, D), C ** -0.5, 0.5, ((2, 32),)),
        "modulator_bias": noise(streams_of[14], (6, D), 0.5, 3.0, ((1, 32),)),
    }


EPS = 1e-05
ROPE_BASE = 10000.0
MASKED = -1e+30
HIGHEST = lax.Precision.HIGHEST

@jax.custom_vjp
def low(v):
    return lax.optimization_barrier(v.astype(jnp.bfloat16)).astype(jnp.float32)

@jax.custom_vjp
def low_back(v):
    return v

def low_keep(v):
    return (low(v), None)

def low_pass(kept, grad):
    return (grad,)

def back_keep(v):
    return (v, None)

def back_low(kept, grad):
    return (low(grad),)
low.defvjp(low_keep, low_pass)
low_back.defvjp(back_keep, back_low)

def modulate(values, weight_gain, offset, stretch):
    center = values - lax.optimization_barrier(jnp.mean(values, axis=-1, keepdims=True))
    second = lax.optimization_barrier(jnp.mean(center * center, axis=-1, keepdims=True))
    return center * lax.rsqrt(second + EPS) * weight_gain * (1.0 + stretch) + offset

def rotary_tables(places, width):
    halfway = width // 2
    inverse = ROPE_BASE ** (-(jnp.arange(halfway, dtype=jnp.float32) * 2.0 / width))
    angles = places.astype(jnp.float32)[:, None] * inverse[None, :]
    return (jnp.cos(angles), jnp.sin(angles))

def rotate(vectors, cosine, sine_part):
    halfway = vectors.shape[-1] // 2
    former = vectors[..., :halfway]
    latter = vectors[..., halfway:]
    cosine = cosine[:, None, :]
    sine_part = sine_part[:, None, :]
    return jnp.concatenate([former * cosine - latter * sine_part, latter * cosine + former * sine_part], axis=-1)

def path_mask(parents, length):
    amount = parents.shape[0]
    labels = jnp.arange(amount, dtype=jnp.int32)
    climb_map = (parents[:, None] == labels[None, :]).astype(jnp.float32)
    identity = jnp.eye(amount, dtype=jnp.float32)

    def climb(iteration, carried):
        reached, ancestry = carried
        reached = jnp.dot(reached, climb_map, precision=HIGHEST)
        return (reached, jnp.maximum(ancestry, reached))
    reached, ancestry = lax.fori_loop(0, amount, climb, (identity, identity))
    linked = jnp.maximum(ancestry, ancestry.T)
    owners = jnp.arange(length, dtype=jnp.int32) // (length // amount)
    chooser = (owners[:, None] == labels[None, :]).astype(jnp.float32)
    joined = jnp.dot(jnp.dot(chooser, linked, precision=HIGHEST), chooser.T, precision=HIGHEST)
    return joined > 0.5

def tree_forward(values, embed_row, parents, places, params):
    gain_first, inlet_weight, outlet_weight, gain_second, up_weight, up_bias, down_weight, down_bias, modulator, modulator_bias = params
    length, width = values.shape
    heads = inlet_weight.shape[2]
    head_width = inlet_weight.shape[3]
    shifts = jnp.dot(jax.nn.silu(embed_row)[None, :], modulator.reshape(modulator.shape[0], -1), precision=HIGHEST).reshape(6, width) + modulator_bias
    normed = low(modulate(values, gain_first, shifts[0], shifts[1]))
    mixed = low_back(jnp.dot(normed, inlet_weight.reshape(width, -1), precision=HIGHEST))
    mixed = mixed.reshape(length, 3, heads, head_width)
    cosine, sine_part = rotary_tables(places, head_width)
    queries = low(rotate(mixed[:, 0], cosine, sine_part))
    keys_rot = low(rotate(mixed[:, 1], cosine, sine_part))
    values_v = low(mixed[:, 2])
    allowed = path_mask(parents, length)
    scores = low_back(jnp.einsum('qhd,khd->hqk', queries, keys_rot, precision=HIGHEST))
    logits = jnp.where(allowed[None], scores * head_width ** (-0.5), MASKED)
    weights = low(jax.nn.softmax(logits, axis=-1))
    attended = jnp.einsum('hqk,khd->qhd', weights, values_v, precision=HIGHEST)
    attended = low(low_back(attended)).reshape(length, width)
    branch = low_back(jnp.dot(attended, outlet_weight.reshape(width, width), precision=HIGHEST))
    middle = values + shifts[2] * branch
    normed_two = low(modulate(middle, gain_second, shifts[3], shifts[4]))
    hidden = low_back(jnp.dot(normed_two, up_weight, precision=HIGHEST) + up_bias)
    activated = low(jax.nn.gelu(hidden, approximate=True))
    mlp_out = low_back(jnp.dot(activated, down_weight, precision=HIGHEST))
    return middle + shifts[5] * (mlp_out + down_bias)

def reference(tokens, cotangent, time_embed, block_parent, positions, gain_first, inlet_weight, outlet_weight, gain_second, up_weight, up_bias, down_weight, down_bias, modulator, modulator_bias):
    params = tuple((member.astype(jnp.float32) for member in (gain_first, inlet_weight, outlet_weight, gain_second, up_weight, up_bias, down_weight, down_bias, modulator, modulator_bias)))
    inputs = tokens.astype(jnp.float32).reshape(TREES, SEQ, D)
    places = positions.reshape(TREES, SEQ)
    embeds = time_embed.astype(jnp.float32)
    stepper = jax.checkpoint(tree_forward)

    def forward(inputs, params):

        def per_tree(carried, member):
            values, embed_row, parents, place_row = member
            return (carried, stepper(values, embed_row, parents, place_row, params))
        carried, outputs = lax.scan(per_tree, jnp.zeros((), jnp.float32), (inputs, embeds, block_parent, places))
        return outputs
    outputs, pullback = jax.vjp(forward, inputs, params)
    token_adj, param_adj = pullback(cotangent.astype(jnp.float32).reshape(TREES, SEQ, D))
    return (outputs.reshape(TREES * SEQ, D).astype(jnp.bfloat16), token_adj.reshape(TREES * SEQ, D).astype(jnp.bfloat16), param_adj[0], param_adj[1], param_adj[2], param_adj[3], param_adj[4], param_adj[5], param_adj[6], param_adj[7], param_adj[8], param_adj[9])
```

```python
from functools import partial

import jax
import jax.numpy as jnp
from jax import lax
from jax.sharding import Mesh, PartitionSpec as P

EPS = 1e-05
ROPE_BASE = 10000.0
MASKED = -1e30
HIGHEST = lax.Precision.HIGHEST


def modulate(values, weight_gain, offset, stretch):
    center = values - jnp.mean(values, axis=-1, keepdims=True)
    second = jnp.mean(center * center, axis=-1, keepdims=True)
    return center * lax.rsqrt(second + EPS) * weight_gain * (1.0 + stretch) + offset


def rotary_tables(places, width):
    halfway = width // 2
    inverse = ROPE_BASE ** (-(jnp.arange(halfway, dtype=jnp.float32) * 2.0 / width))
    angles = places.astype(jnp.float32)[:, None] * inverse[None, :]
    return (jnp.cos(angles), jnp.sin(angles))


def rotate(vectors, cosine, sine_part):
    halfway = vectors.shape[-1] // 2
    former = vectors[..., :halfway]
    latter = vectors[..., halfway:]
    cosine = cosine[:, None, :]
    sine_part = sine_part[:, None, :]
    return jnp.concatenate(
        [former * cosine - latter * sine_part, latter * cosine + former * sine_part], axis=-1
    )


def family(climb_map, labels):
    amount = climb_map.shape[0]
    proper = climb_map * (labels[:, None] != labels[None, :])
    reached = proper
    ancestry = proper
    for _ in range(2):
        reached = jnp.dot(reached, proper, precision=HIGHEST)
        ancestry = ancestry + reached
    depth = jnp.sum(ancestry, axis=1)
    return depth, ancestry + ancestry.T + jnp.eye(amount, dtype=jnp.float32)


def head_order(array):
    return jnp.transpose(array, (1, 0, 2))


def head_forward(allowed, scale_factor, bundle):
    queries, keys_rot, values_v = bundle
    scores = jnp.dot(queries, keys_rot.T, preferred_element_type=jnp.float32)
    logits = jnp.where(allowed, scores * scale_factor, MASKED)
    highest = jnp.max(logits, axis=-1, keepdims=True)
    raised = jnp.exp(logits - highest)
    totals = jnp.sum(raised, axis=-1, keepdims=True)
    probs = raised / totals
    attended = jnp.dot(probs.astype(jnp.bfloat16), values_v, preferred_element_type=jnp.float32)
    return (attended.astype(jnp.bfloat16), (highest + jnp.log(totals))[:, 0])


def head_backward(allowed, scale_factor, bundle):
    queries, keys_rot, values_v, slope, log_total = bundle
    scores = jnp.dot(queries, keys_rot.T, preferred_element_type=jnp.float32)
    logits = jnp.where(allowed, scores * scale_factor, MASKED)
    probs = jnp.exp(logits - log_total[:, None])
    value_adj = jnp.dot(probs.astype(jnp.bfloat16).T, slope, preferred_element_type=jnp.float32)
    prob_slope = jnp.dot(slope, values_v.T, preferred_element_type=jnp.float32)
    inner = jnp.sum(probs * prob_slope, axis=-1, keepdims=True)
    score_slope = (probs * (prob_slope - inner) * scale_factor).astype(jnp.bfloat16)
    query_adj = jnp.dot(score_slope, keys_rot, preferred_element_type=jnp.float32)
    key_adj = jnp.dot(score_slope.T, queries, preferred_element_type=jnp.float32)
    return (query_adj, key_adj, value_adj)


ALL = ("chip", "core", "tensor")
CROSS = ("core", "tensor")
DIAGONAL = [(0, 0), (1, 2), (2, 1), (3, 3)]
TURN = [(1, 0), (0, 2), (2, 3), (3, 1)]
TURN_BACK = [(0, 1), (2, 0), (3, 2), (1, 3)]


def diagonal(array):
    return lax.ppermute(array, CROSS, DIAGONAL)


def other_core(array):
    return lax.ppermute(array, "core", [(0, 1), (1, 0)])


def chip_masks(chips):
    masks = []
    mask = chips // 2
    while mask:
        masks.append(mask)
        mask //= 2
    return masks


def partner(array, mask, chips):
    return lax.ppermute(array, "chip", [(i, i ^ mask) for i in range(chips)])


def gather_shards(shard, chips):
    held = jnp.stack([diagonal(shard), lax.ppermute(shard, CROSS, TURN_BACK)])
    for mask in chip_masks(chips):
        held = jnp.concatenate([held, partner(held, mask, chips)], axis=0)
    return held


def scatter_shards(blocks, chips, on_diagonal):
    low = jnp.bfloat16
    for mask in reversed(chip_masks(chips)):
        half = blocks.shape[0] // 2
        arrived = partner(blocks[half:].astype(low), mask, chips)
        blocks = blocks[:half] + arrived.astype(jnp.float32)
    mine, turned = blocks[0], blocks[1]
    straight = diagonal(mine.astype(low)).astype(jnp.float32)
    arrived = lax.ppermute(turned.astype(low), CROSS, TURN).astype(jnp.float32)
    return jnp.where(on_diagonal, mine, straight) + arrived


def block_owners(chips):
    places = [0, 1]
    for mask in chip_masks(chips):
        places = places + [place ^ (2 * mask) for place in places]
    return places


def exchange_small(rows):
    return lax.all_to_all(rows, ALL, split_axis=0, concat_axis=0, tiled=True)


def per_device(
    chips,
    tokens,
    cotangent,
    time_embed,
    block_parent,
    positions,
    gain_first,
    inlet_weight,
    outlet_weight,
    gain_second,
    up_weight,
    up_bias,
    down_weight,
    down_bias,
    modulator,
    modulator_bias,
):
    f32 = jnp.float32
    low = jnp.bfloat16
    devices = chips * 4
    trees = chips * 2
    own_rows, width = tokens.shape
    slim = gain_first.shape[0]
    units = up_bias.shape[0]
    local_heads = inlet_weight.shape[2]
    head_width = inlet_weight.shape[3]
    core = lax.axis_index("core")
    side = lax.axis_index("tensor")
    on_diagonal = core == side
    me = lax.axis_index("chip") * 2 + side
    order = block_owners(chips)
    owners = me ^ jnp.array(order, dtype=jnp.int32)
    spots = jnp.take(
        jnp.array([order.index(i) for i in range(trees)], dtype=jnp.int32),
        me ^ jnp.arange(trees, dtype=jnp.int32),
    )

    small = jnp.concatenate([time_embed[0], block_parent[0].astype(f32)])
    amount = block_parent.shape[1]
    every_embed = exchange_small(
        jnp.broadcast_to(small[None, :], (devices, small.shape[0]))
    ).reshape(trees, 2, -1)[:, 0]
    embeds = every_embed[:, : time_embed.shape[1]]
    tree_row = lax.dynamic_index_in_dim(every_embed, me, 0, keepdims=False)
    parents = tree_row[time_embed.shape[1] :].astype(jnp.int32)
    embeds_act = jax.nn.silu(embeds)
    slices = jnp.dot(
        embeds_act, modulator.astype(f32).reshape(modulator.shape[0], -1), precision=HIGHEST
    ) + modulator_bias.astype(f32).reshape(1, -1)
    slices = jnp.broadcast_to(
        slices.reshape(chips, 1, 2, 6 * slim), (chips, 2, 2, 6 * slim)
    ).reshape(devices, 6 * slim)
    vectors = jnp.concatenate([gain_first, gain_second, down_bias, up_bias]).astype(f32)
    arrived = exchange_small(
        jnp.concatenate(
            [slices, jnp.broadcast_to(vectors[None, :], (devices, vectors.shape[0]))], axis=1
        )
    )
    shifts = (
        arrived[:, : 6 * slim].reshape(devices, 6, slim).transpose(1, 0, 2).reshape(6, width)
    )
    norm_one = arrived[:, 6 * slim : 7 * slim].reshape(width)
    norm_two = arrived[:, 7 * slim : 8 * slim].reshape(width)
    bias_down = arrived[:, 8 * slim : 9 * slim].reshape(width)
    bias_rows = lax.dynamic_index_in_dim(
        arrived[:, 9 * slim :].reshape(trees, 2, units), core, 1, keepdims=False
    )
    up_bias_full = jnp.take(bias_rows, owners, axis=0).reshape(-1)

    inlet_rel = gather_shards(inlet_weight.reshape(inlet_weight.shape[0], -1), chips)
    inlet_flat = jnp.take(inlet_rel, spots, axis=0).reshape(width, -1)
    outlet_rel = gather_shards(outlet_weight.reshape(-1, outlet_weight.shape[2]).T, chips)
    outlet_turned = jnp.take(outlet_rel, spots, axis=0).reshape(width, -1)
    up_turned = gather_shards(up_weight.T, chips).reshape(-1, width)
    down_full = gather_shards(down_weight, chips).reshape(-1, width)

    values = diagonal(tokens).astype(f32)
    slope = diagonal(cotangent).astype(f32)

    def both(array):
        return jnp.concatenate([array, other_core(array)], axis=0)

    def shared(part):
        return part[:own_rows] + other_core(part[own_rows:].astype(low)).astype(f32)

    normed = modulate(values, norm_one, shifts[0], shifts[1]).astype(low)
    normed_all = both(normed)
    length = normed_all.shape[0]
    mixed = jnp.dot(normed_all, inlet_flat, preferred_element_type=f32).reshape(
        length, 3, local_heads, head_width
    )
    labels = jnp.arange(amount, dtype=jnp.int32)
    climb_map = (parents[:, None] == labels[None, :]).astype(f32)
    block_rows = (labels + core * (amount // 2)) % amount
    depth, linked = family(climb_map, labels)
    block = length // amount
    depth_rows = jnp.take(depth, block_rows)
    places = (depth_rows[:, None] * block + jnp.arange(block, dtype=f32)[None, :]).reshape(-1)
    cosine, sine_part = rotary_tables(places, head_width)
    queries = head_order(rotate(mixed[:, 0], cosine, sine_part).astype(low))
    keys_rot = head_order(rotate(mixed[:, 1], cosine, sine_part).astype(low))
    values_v = head_order(mixed[:, 2].astype(low))
    linked = jnp.take(jnp.take(linked, block_rows, axis=0), block_rows, axis=1)
    allowed = jnp.repeat(jnp.repeat(linked > 0.5, block, axis=0), block, axis=1)
    scale_factor = head_width ** (-0.5)
    attended_heads, log_totals = lax.map(
        partial(head_forward, allowed, scale_factor), (queries, keys_rot, values_v)
    )
    attended = head_order(attended_heads).reshape(length, local_heads * head_width)
    branch = shared(
        lax.dot_general(
            attended, outlet_turned, (((1,), (1,)), ((), ())), preferred_element_type=f32
        )
    )
    middle = values + shifts[2] * branch
    normed_two = modulate(middle, norm_two, shifts[3], shifts[4]).astype(low)
    normed_two_all = both(normed_two)
    hidden = (
        lax.dot_general(
            normed_two_all, up_turned, (((1,), (1,)), ((), ())), preferred_element_type=f32
        )
        + up_bias_full
    )
    activated = jax.nn.gelu(hidden, approximate=True).astype(low)
    mlp_out = shared(jnp.dot(activated, down_full, preferred_element_type=f32))
    layer_output = diagonal((middle + shifts[5] * (mlp_out + bias_down)).astype(low))

    gate_two_adj = jnp.sum(slope * (mlp_out + bias_down), axis=0)
    down_bias_adj = jnp.sum(slope, axis=0) * shifts[5]
    mlp_slope_all = both((slope * shifts[5]).astype(low))
    act_slope = lax.dot_general(
        mlp_slope_all, down_full, (((1,), (1,)), ((), ())), preferred_element_type=f32
    )
    down_adj = lax.dot_general(
        activated, mlp_slope_all, (((0,), (0,)), ((), ())), preferred_element_type=f32
    )
    down_share = scatter_shards(down_adj.reshape(trees, -1, width), chips, on_diagonal)
    gelu_back = jax.vjp(partial(jax.nn.gelu, approximate=True), hidden)[1]
    hidden_slope = gelu_back(act_slope)[0].astype(low)
    up_bias_adj = jnp.sum(hidden_slope.astype(f32), axis=0)
    norm_two_part = jnp.dot(hidden_slope, up_turned, preferred_element_type=f32)
    up_adj = lax.dot_general(
        hidden_slope, normed_two_all, (((0,), (0,)), ((), ())), preferred_element_type=f32
    )
    up_share = scatter_shards(up_adj.reshape(trees, -1, width), chips, on_diagonal).T
    norm_two_slope = shared(norm_two_part)
    middle_back = jax.vjp(modulate, middle, norm_two, shifts[3], shifts[4])[1]
    middle_adj, gain_two_adj, shift_two_adj, scale_two_adj = middle_back(norm_two_slope)
    middle_slope = slope + middle_adj
    gate_one_adj = jnp.sum(middle_slope * branch, axis=0)
    branch_slope_all = both((middle_slope * shifts[2]).astype(low))
    attended_slope = jnp.dot(
        branch_slope_all, outlet_turned, preferred_element_type=f32
    ).astype(low)
    outlet_adj = lax.dot_general(
        branch_slope_all, attended, (((0,), (0,)), ((), ())), preferred_element_type=f32
    )
    outlet_share = scatter_shards(
        jnp.take(outlet_adj.reshape(trees, -1, outlet_adj.shape[1]), owners, axis=0),
        chips,
        on_diagonal,
    )
    outlet_share = outlet_share.T.reshape(local_heads, head_width, -1)
    attended_slope = head_order(attended_slope.reshape(length, local_heads, head_width))
    query_adj, key_adj, value_adj = lax.map(
        partial(head_backward, allowed, scale_factor),
        (queries, keys_rot, values_v, attended_slope, log_totals),
    )
    query_adj = rotate(head_order(query_adj), cosine, -sine_part)
    key_adj = rotate(head_order(key_adj), cosine, -sine_part)
    mixed_slope = (
        jnp.stack([query_adj, key_adj, head_order(value_adj)], axis=1)
        .astype(low)
        .reshape(length, -1)
    )
    inlet_adj = lax.dot_general(
        normed_all, mixed_slope, (((0,), (0,)), ((), ())), preferred_element_type=f32
    )
    inlet_share = scatter_shards(
        jnp.take(inlet_adj.reshape(trees, -1, inlet_adj.shape[1]), owners, axis=0),
        chips,
        on_diagonal,
    ).reshape(-1, 3, local_heads, head_width)
    normed_slope = shared(
        lax.dot_general(
            mixed_slope, inlet_flat, (((1,), (1,)), ((), ())), preferred_element_type=f32
        )
    )
    values_back = jax.vjp(modulate, values, norm_one, shifts[0], shifts[1])[1]
    values_adj, gain_one_adj, shift_one_adj, scale_one_adj = values_back(normed_slope)
    adjoint_tokens = diagonal((middle_slope + values_adj).astype(low))
    sums = jnp.stack(
        [
            shift_one_adj,
            scale_one_adj,
            gate_one_adj,
            shift_two_adj,
            scale_two_adj,
            gate_two_adj,
            gain_one_adj,
            gain_two_adj,
            down_bias_adj,
        ]
    )
    sums = sums.reshape(9, devices, slim).transpose(1, 0, 2).reshape(devices, 9 * slim)
    bias_rows = jnp.take(up_bias_adj.reshape(trees, units), spots, axis=0)
    bias_rows = jnp.where(
        jnp.arange(2)[None, :, None] == core, bias_rows[:, None, :], 0.0
    ).reshape(devices, units)
    back = exchange_small(jnp.concatenate([sums, bias_rows], axis=1)).reshape(
        chips, 2, 2, 9 * slim + units
    )
    dmods = jnp.sum(back[..., : 6 * slim], axis=1).reshape(trees, 6 * slim)
    rest = jnp.sum(back[..., 6 * slim :].reshape(devices, -1), axis=0)
    mod_bias_share = jnp.sum(dmods, axis=0).reshape(6, slim)
    mod_weight_share = lax.dot_general(
        embeds_act, dmods, (((0,), (0,)), ((), ())), precision=HIGHEST
    ).reshape(-1, 6, slim)
    return (
        layer_output,
        adjoint_tokens,
        rest[:slim],
        inlet_share,
        outlet_share,
        rest[slim : 2 * slim],
        up_share,
        rest[3 * slim :],
        down_share,
        rest[2 * slim : 3 * slim],
        mod_weight_share,
        mod_bias_share,
    )


def solution(mesh):
    chips = mesh.shape["dp"] // 2
    whole = Mesh(mesh.devices.reshape(chips, 2, mesh.shape["tensor"]), ALL)
    dp = ("chip", "core")
    in_specs = (
        P(ALL, None),
        P(ALL, None),
        P(dp, None),
        P(dp, None),
        P(dp),
        P(ALL),
        P(dp, None, "tensor", None),
        P("tensor", None, dp),
        P(ALL),
        P(None, ALL),
        P(ALL),
        P(ALL, None),
        P(ALL),
        P(None, None, ALL),
        P(None, ALL),
    )
    out_specs = (
        P(ALL, None),
        P(ALL, None),
        P(ALL),
        P(dp, None, "tensor", None),
        P("tensor", None, dp),
        P(ALL),
        P(None, ALL),
        P(ALL),
        P(ALL, None),
        P(ALL),
        P(None, None, ALL),
        P(None, ALL),
    )
    return jax.shard_map(
        partial(per_device, chips),
        mesh=whole,
        in_specs=in_specs,
        out_specs=out_specs,
        check_vma=False,
    )
```
